32 devices in a mesh: replica: 8 (over y, x, core), shard: 4 (over z).
Axes of the slice: x: 2, y: 2, z: 4, core: 2. Of those that a mesh axis runs over, the one named last changes fastest.
Arguments:
- tokens: bfloat16 [32768, 1024], P(('replica', 'shard')), may hold values from -6 to 6
- seq_start: int32 [32], P(('replica', 'shard')), may hold values from 0 to 1024, as said below
- out_grad: bfloat16 [32768, 1024], P(('replica', 'shard')), may hold values from -6 to 6
- norm_gain: bfloat16 [1024], P('shard'), may hold values from 0.099609375 to 1.8984375
- w_query: bfloat16 [1024, 512], P('shard'), may hold values from -0.1875 to 0.1875
- w_key: bfloat16 [1024, 512], P('shard'), may hold values from -0.1875 to 0.1875
- w_value: bfloat16 [1024, 1024], P('shard'), may hold values from -0.1875 to 0.1875
- w_outgate: bfloat16 [1024, 1024], P('shard'), may hold values from -0.1875 to 0.1875
- w_lowrank: bfloat16 [1024, 16], P('shard'), may hold values from -0.1875 to 0.1875
- w_rank_up: bfloat16 [16, 512], P('shard'), may hold values from -1.5 to 1.5
- gate_bias: bfloat16 [512], P('shard'), may hold values from 0 to 9
- head_gain: bfloat16 [256], P('shard'), may hold values from 0.099609375 to 1.8984375
- w_output: bfloat16 [1024, 1024], P('shard'), may hold values from -0.1875 to 0.1875
- ffn_gain: bfloat16 [1024], P('shard'), may hold values from 0.099609375 to 1.8984375
- w_gate: bfloat16 [1024, 2816], P('shard'), may hold values from -0.1875 to 0.1875
- w_up: bfloat16 [1024, 2816], P('shard'), may hold values from -0.1875 to 0.1875
- w_down: bfloat16 [2816, 1024], P('shard'), may hold values from -0.109375 to 0.109375
Outputs:
- output: bfloat16 [32768, 1024], P(('replica', 'shard'))
- tokens_grad: bfloat16 [32768, 1024], P(('replica', 'shard'))
- norm_gain_grad: float32 [1024], P('shard')
- w_query_grad: float32 [1024, 512], P('shard')
- w_key_grad: float32 [1024, 512], P('shard')
- w_value_grad: float32 [1024, 1024], P('shard')
- w_outgate_grad: float32 [1024, 1024], P('shard')
- w_lowrank_grad: float32 [1024, 16], P('shard')
- w_rank_up_grad: float32 [16, 512], P('shard')
- gate_bias_grad: float32 [512], P('shard')
- head_gain_grad: float32 [256], P('shard')
- w_output_grad: float32 [1024, 1024], P('shard')
- ffn_gain_grad: float32 [1024], P('shard')
- w_gate_grad: float32 [1024, 2816], P('shard')
- w_up_grad: float32 [1024, 2816], P('shard')
- w_down_grad: float32 [2816, 1024], P('shard')
The draws below stay inside these ranges and needn't reach their ends.
Inputs may be any that keep to these rules, and one draw needn't show every extreme that they name: `seq_start`: 1024 means that no sequence begins on the device; other values are multiples of 64; the first device holds 0; sequences begin only on devices whose index along replica+shard is a multiple of 4, and some of those devices hold no start, so that a sequence may run through several groups of 4 devices.
All inputs are finite; a program needn't handle non-finite values.
Results may differ from the reference program's by a relative error of at most 0.025.
Values may be sent and summed in bfloat16 or wider, within the bound.
A program may use at most 640 MiB of HBM per device.

```python
import jax
import jax.numpy as jnp
from jax import lax

D = 1024
HEAD_COUNT = 4
DK = 128
VALUE_WIDTH = 256
FF = 2816
RANK = 16
BLOCK = 64
SPAN = 4
TOK_DEV = 1024
KD = 512
VD = 1024
TOKENS = 32768
DEVICES = 32


def draw_seq_start(key, part):
    device_ids = jnp.arange(DEVICES, dtype=jnp.int32)
    offsets = jax.random.randint(jax.random.fold_in(key, 1), (DEVICES,), 0, TOK_DEV // BLOCK, dtype=jnp.int32) * BLOCK
    group_total = DEVICES // SPAN
    ranks = jax.random.permutation(jax.random.fold_in(key, 2), group_total).astype(jnp.int32)
    silent_groups = max(1, group_total // 4)
    silent = jnp.repeat(ranks < silent_groups, SPAN)
    starts = jnp.where(jnp.logical_and(device_ids % SPAN == 0, jnp.logical_not(silent)), offsets, TOK_DEV)
    return jnp.where(device_ids == 0, 0, starts).astype(jnp.int32)


def levels(stream_key, shape, split, smallest, high):
    def one(axis_at, blocks):
        steps = jax.random.uniform(jax.random.fold_in(jax.random.fold_in(stream_key, 6), axis_at), (blocks,), jnp.float32, smallest / len(split), high / len(split))
        return jnp.repeat(jnp.exp(steps), shape[axis_at] // blocks).reshape((-1,) + (1,) * (len(shape) - axis_at - 1))

    level = one(*split[0])
    for cut in split[1:]:
        level = level * one(*cut)
    return level


def bell_draw(rng, shape, width, reach, shards=(), kind=jnp.bfloat16):
    array = jax.random.normal(rng, shape, jnp.float32) * width
    if len(shards) > 0:
        array = levels(rng, shape, shards, -0.22, 0.18) * array
    return jnp.clip(array, min=-reach, max=reach).astype(kind)


def setup_inputs(seed: int = 0) -> dict:
    arg_keys = jax.random.split(jax.random.key(seed), 18)
    return {
        "tokens": bell_draw(arg_keys[0], (TOKENS, D), 1.0, 6.0, ((0, 32),)),
        "seq_start": draw_seq_start(jax.random.fold_in(arg_keys[17], 71), 0),
        "out_grad": bell_draw(arg_keys[2], (TOKENS, D), 1.0, 6.0, ((0, 32),)),
        "norm_gain": jnp.clip(1.0 + 0.18 * jax.random.normal(arg_keys[3], (D,), jnp.float32), 0.099609375, 1.8984375).astype(jnp.bfloat16),
        "w_query": bell_draw(arg_keys[4], (D, KD), D ** -0.5, 0.1875, ((0, 4),)),
        "w_key": bell_draw(arg_keys[5], (D, KD), D ** -0.5, 0.1875, ((0, 4),)),
        "w_value": bell_draw(arg_keys[6], (D, VD), D ** -0.5, 0.1875, ((0, 4),)),
        "w_outgate": bell_draw(arg_keys[7], (D, VD), D ** -0.5, 0.1875, ((0, 4),)),
        "w_lowrank": bell_draw(arg_keys[8], (D, RANK), D ** -0.5, 0.1875, ((0, 4),)),
        "w_rank_up": bell_draw(arg_keys[9], (RANK, KD), RANK ** -0.5, 1.5, ((0, 4),)),
        "gate_bias": jnp.clip(9.0 * jax.random.uniform(arg_keys[10], (KD,), jnp.float32) ** levels(arg_keys[10], (KD,), ((0, 4),), -0.2, 0.2), 0.0, 9.0).astype(jnp.bfloat16),
        "head_gain": jnp.clip(1.0 + 0.18 * jax.random.normal(arg_keys[11], (VALUE_WIDTH,), jnp.float32), 0.099609375, 1.8984375).astype(jnp.bfloat16),
        "w_output": bell_draw(arg_keys[12], (VD, D), VD ** -0.5, 0.1875, ((0, 4),)),
        "ffn_gain": jnp.clip(1.0 + 0.18 * jax.random.normal(arg_keys[13], (D,), jnp.float32), 0.099609375, 1.8984375).astype(jnp.bfloat16),
        "w_gate": bell_draw(arg_keys[14], (D, FF), D ** -0.5, 0.1875, ((0, 4),)),
        "w_up": bell_draw(arg_keys[15], (D, FF), D ** -0.5, 0.1875, ((0, 4),)),
        "w_down": bell_draw(arg_keys[16], (FF, D), FF ** -0.5, 0.109375, ((0, 4),)),
    }


@jax.custom_vjp
def low(v):
    return lax.optimization_barrier(v.astype(jnp.bfloat16)).astype(jnp.float32)

@jax.custom_vjp
def low_back(v):
    return v

def low_keep(v):
    return (low(v), None)

def low_pass(kept, grad):
    return (grad,)

def back_keep(v):
    return (v, None)

def back_low(kept, grad):
    return (low(grad),)
low.defvjp(low_keep, low_pass)
low_back.defvjp(back_keep, back_low)
epsilon = 1e-05
normalizer = 16.0
highest_precision = lax.Precision.HIGHEST

def product(left, right):
    return jnp.dot(left, right, precision=highest_precision, preferred_element_type=jnp.float32)

def rms_norm(values, gain):
    return values * lax.rsqrt(lax.optimization_barrier(jnp.mean(values * values, axis=-1, keepdims=True)) + epsilon) * gain

def output_gate(mixed_rows, outgate, head_gain):
    count_of_rows = mixed_rows.shape[0]
    shaped = rms_norm(mixed_rows.reshape(count_of_rows, HEAD_COUNT, VALUE_WIDTH), head_gain).reshape(count_of_rows, HEAD_COUNT * VALUE_WIDTH)
    return shaped * jax.nn.silu(outgate)

def block_step(entering_state, inputs):
    query_rows, key_rows, rows_of_value, log_decay, reset = inputs
    entering_state = entering_state * (1.0 - reset)
    cumul = jnp.cumsum(log_decay, axis=0)
    block_stop = cumul[-1]
    query_decayed = query_rows * jnp.exp(cumul)
    key_dec = key_rows * jnp.exp(-cumul)
    key_final_decay = key_rows * jnp.exp(block_stop - cumul)
    inter_block_part = jnp.einsum('gqs,qso->gqo', query_decayed, entering_state, precision=highest_precision)
    scores = jnp.einsum('ihk,jhk->hij', query_decayed, key_dec, precision=highest_precision)
    causal = jnp.tril(jnp.ones((BLOCK, BLOCK), jnp.float32))
    intra_part = jnp.einsum('hij,jhv->ihv', scores * causal, rows_of_value, precision=highest_precision)
    leaving_state = jnp.exp(block_stop)[:, :, None] * entering_state + jnp.einsum('are,aro->reo', key_final_decay, rows_of_value, precision=highest_precision)
    return (leaving_state, inter_block_part + intra_part)

def mixer(query_rows, key_rows, rows_of_value, log_decay, resets, entering_state):
    count_of_rows = query_rows.shape[0]
    block_count = count_of_rows // BLOCK
    shaped = (query_rows.reshape(block_count, BLOCK, HEAD_COUNT, DK), key_rows.reshape(block_count, BLOCK, HEAD_COUNT, DK), rows_of_value.reshape(block_count, BLOCK, HEAD_COUNT, VALUE_WIDTH), log_decay.reshape(block_count, BLOCK, HEAD_COUNT, DK), resets)
    leaving_state, mixed = lax.scan(jax.checkpoint(block_step), entering_state, shaped)
    return (mixed.reshape(count_of_rows, HEAD_COUNT * VALUE_WIDTH), leaving_state)

def layer_rows(weights, entering_state, inputs):
    norm_gain, w_query, w_key, w_value, w_outgate, w_lowrank, w_rank_up, gate_bias, head_gain, w_output, ffn_gain, w_gate, w_up, w_down = weights
    residual_in, resets = inputs
    normed = low(rms_norm(residual_in, norm_gain))
    query_rows = low_back(low(product(normed, w_query)))
    key_rows = low_back(low(product(normed, w_key)))
    rows_of_value = low_back(low(product(normed, w_value)))
    outgate = low_back(product(normed, w_outgate))
    rank_rows = low_back(low(product(normed, w_lowrank)))
    gate_logit = low_back(product(rank_rows, w_rank_up) + gate_bias)
    log_decay = jax.nn.log_sigmoid(gate_logit) / normalizer
    mixed_rows, leaving_state = mixer(query_rows, key_rows, rows_of_value, log_decay, resets, entering_state)
    gated_rows = low(output_gate(mixed_rows, outgate, head_gain))
    middle = residual_in + low_back(product(gated_rows, w_output))
    normed_ffn = low(rms_norm(middle, ffn_gain))
    gate_pre = low_back(product(normed_ffn, w_gate))
    up_pre = low_back(product(normed_ffn, w_up))
    hidden = low(jax.nn.silu(gate_pre) * up_pre)
    return (leaving_state, middle + low_back(product(hidden, w_down)))

def forward(weights, residual_all, resets):
    group_rows = 4 * TOK_DEV
    groups_count = residual_all.shape[0] // group_rows

    def step_rows(entering_state, inputs):
        return jax.checkpoint(layer_rows)(weights, entering_state, inputs)
    initial = jnp.zeros((HEAD_COUNT, DK, VALUE_WIDTH), jnp.float32)
    final, produced = lax.scan(step_rows, initial, (residual_all.reshape(groups_count, group_rows, D), resets.reshape(groups_count, group_rows // BLOCK)))
    return produced.reshape(groups_count * group_rows, D)

def reference(tokens, seq_start, out_grad, norm_gain, w_query, w_key, w_value, w_outgate, w_lowrank, w_rank_up, gate_bias, head_gain, w_output, ffn_gain, w_gate, w_up, w_down):
    weights = tuple((weight.astype(jnp.float32) for weight in (norm_gain, w_query, w_key, w_value, w_outgate, w_lowrank, w_rank_up, gate_bias, head_gain, w_output, ffn_gain, w_gate, w_up, w_down)))
    local_blocks = TOK_DEV // BLOCK
    offsets = jnp.arange(local_blocks, dtype=jnp.int32) * BLOCK
    resets = (offsets[None, :] == seq_start.astype(jnp.int32)[:, None]).astype(jnp.float32).reshape(-1)

    def whole(weight_set, residual_all):
        return forward(weight_set, residual_all, resets)
    produced, pull = jax.vjp(whole, weights, tokens.astype(jnp.float32))
    weight_grads, token_grad = pull(out_grad.astype(jnp.float32))
    return (produced.astype(jnp.bfloat16), token_grad.astype(jnp.bfloat16), weight_grads[0], weight_grads[1], weight_grads[2], weight_grads[3], weight_grads[4], weight_grads[5], weight_grads[6], weight_grads[7], weight_grads[8], weight_grads[9], weight_grads[10], weight_grads[11], weight_grads[12], weight_grads[13])
```

```python
import jax
import jax.numpy as jnp
from jax import lax
from jax.experimental import pallas as pl
from jax.experimental.pallas import tpu as pltpu
from jax.sharding import PartitionSpec as P

HEAD_COUNT = 4
DK = 128
VALUE_WIDTH = 256
BLOCK = 64
KD = HEAD_COUNT * DK
VD = HEAD_COUNT * VALUE_WIDTH
EVERY = ("replica", "shard")
ROWS = ("shard", "replica")
SIDE = 128

epsilon = 1e-05
normalizer = 16.0
highest = lax.Precision.HIGHEST
high = lax.Precision.HIGH


def dense(left, right):
    return jnp.dot(left, right, preferred_element_type=jnp.float32)


def dense_back(grad_rows, weight):
    return lax.dot_general(
        grad_rows, weight, (((1,), (1,)), ((), ())), preferred_element_type=jnp.float32
    )


def dense_left(input_rows, grad_rows):
    return lax.dot_general(
        input_rows, grad_rows, (((0,), (0,)), ((), ())), preferred_element_type=jnp.float32
    )


def rms_norm(values, gain):
    return values * lax.rsqrt(jnp.mean(values * values, axis=-1, keepdims=True) + epsilon) * gain


def output_gate(mixed_rows, outgate, head_gain):
    count_of_rows = mixed_rows.shape[0]
    shaped = rms_norm(
        mixed_rows.reshape(count_of_rows, HEAD_COUNT, VALUE_WIDTH), head_gain
    ).reshape(count_of_rows, HEAD_COUNT * VALUE_WIDTH)
    return shaped * jax.nn.silu(outgate)


def swiglu(gate_pre, up_pre):
    return jax.nn.silu(gate_pre) * up_pre


def halves(a):
    if a.dtype == jnp.bfloat16:
        return (a, None)
    top = a.astype(jnp.bfloat16)
    return (top, (a - top.astype(jnp.float32)).astype(jnp.bfloat16))


def product(left, right, dims):
    def one(a, b):
        return lax.dot_general(a, b, (dims, ((), ())), preferred_element_type=jnp.float32)

    total = one(left[0], right[0])
    if left[1] is not None:
        total = total + one(left[1], right[0])
    if right[1] is not None:
        total = total + one(left[0], right[1])
    return total


def exact(left, right):
    return lax.dot_general(
        left, right, (NT, ((), ())), precision=highest, preferred_element_type=jnp.float32
    )


NN = ((1,), (0,))
NT = ((1,), (1,))
TN = ((0,), (0,))


def causal_mask():
    rows = lax.broadcasted_iota(jnp.int32, (BLOCK, BLOCK), 0)
    cols = lax.broadcasted_iota(jnp.int32, (BLOCK, BLOCK), 1)
    return rows >= cols


def forward_kernel(start_ref, qkv_ref, cumul_ref, incoming_ref, mixed_ref, saved_ref, state_ref):
    block = pl.program_id(0)

    @pl.when(block == 0)
    def _():
        state_ref[...] = incoming_ref[...].astype(jnp.float32)

    keep = jnp.where(block * BLOCK == start_ref[0], 0.0, 1.0)
    causal = causal_mask()
    for h in range(HEAD_COUNT):
        ks = slice(h * DK, (h + 1) * DK)
        vs = slice(h * VALUE_WIDTH, (h + 1) * VALUE_WIDTH)
        query = qkv_ref[:, ks].astype(jnp.float32)
        key = qkv_ref[:, KD + h * DK : KD + (h + 1) * DK].astype(jnp.float32)
        value = qkv_ref[:, 2 * KD + h * VALUE_WIDTH : 2 * KD + (h + 1) * VALUE_WIDTH]
        cumul = cumul_ref[:, ks]
        stop = cumul[BLOCK - 1 :, :]
        state = state_ref[vs, :] * keep
        saved_ref[0, vs, :] = state
        query_f = query * jnp.exp(cumul)
        key_f = key * jnp.exp(-cumul)
        query_dec = halves(query_f)
        key_end = halves(key * jnp.exp(stop - cumul))
        scores = jnp.where(causal, exact(query_f, key_f), 0.0)
        mixed_ref[:, vs] = product(query_dec, halves(state), NT) + product(
            halves(scores), (value, None), NN
        )
        state_ref[vs, :] = state * jnp.exp(stop) + product((value, None), key_end, TN)


def backward_kernel(
    start_ref, qkv_ref, cumul_ref, grad_ref, saved_ref, outgoing_ref, gqkv_ref, gdecay_ref, back_ref
):
    step = pl.program_id(0)
    block = pl.num_programs(0) - 1 - step

    @pl.when(step == 0)
    def _():
        back_ref[...] = outgoing_ref[...].astype(jnp.float32)

    keep = jnp.where(block * BLOCK == start_ref[0], 0.0, 1.0)
    causal = causal_mask()
    suffix = jnp.where(
        lax.broadcasted_iota(jnp.int32, (BLOCK, BLOCK), 0)
        <= lax.broadcasted_iota(jnp.int32, (BLOCK, BLOCK), 1),
        1.0,
        0.0,
    )
    last = lax.broadcasted_iota(jnp.int32, (BLOCK, DK), 0) == BLOCK - 1
    for h in range(HEAD_COUNT):
        ks = slice(h * DK, (h + 1) * DK)
        ks2 = slice(KD + h * DK, KD + (h + 1) * DK)
        vs = slice(h * VALUE_WIDTH, (h + 1) * VALUE_WIDTH)
        vs2 = slice(2 * KD + h * VALUE_WIDTH, 2 * KD + (h + 1) * VALUE_WIDTH)
        query = qkv_ref[:, ks].astype(jnp.float32)
        key = qkv_ref[:, ks2].astype(jnp.float32)
        value = (qkv_ref[:, vs2], None)
        cumul = cumul_ref[:, ks]
        stop = cumul[BLOCK - 1 :, :]
        grow = jnp.exp(cumul)
        shrink = jnp.exp(-cumul)
        to_end = jnp.exp(stop - cumul)
        whole = jnp.exp(stop)
        query_f = query * grow
        key_f = key * shrink
        end_f = key * to_end
        query_dec = halves(query_f)
        key_dec = halves(key_f)
        key_end = halves(end_f)
        grad_f = grad_ref[:, vs]
        grad = halves(grad_f)
        rest = (grad_f - grad[0].astype(jnp.float32)) - grad[1].astype(jnp.float32)
        grad_value = product(grad, value, NT) + product(
            (rest.astype(jnp.bfloat16), None), value, NT
        )
        state_f = saved_ref[0, vs, :]
        back_f = back_ref[vs, :]
        state = halves(state_f)
        back = halves(back_f)
        scores = halves(jnp.where(causal, product(query_dec, key_dec, NT), 0.0))
        pull = halves(jnp.where(causal, grad_value, 0.0))
        g_query_dec = product(grad, state, NN) + product(pull, key_dec, NN)
        g_key_dec = product(pull, query_dec, TN)
        g_key_end = product(value, back, NN)
        g_value = product(scores, grad, TN) + product(key_end, back, NT)
        gqkv_ref[:, ks] = (g_query_dec * grow).astype(jnp.bfloat16)
        gqkv_ref[:, ks2] = (g_key_dec * shrink + g_key_end * to_end).astype(jnp.bfloat16)
        gqkv_ref[:, vs2] = g_value.astype(jnp.bfloat16)
        end_part = g_key_end * end_f
        at_stop = jnp.sum(end_part, axis=0, keepdims=True) + whole * jnp.sum(
            state_f * back_f, axis=0, keepdims=True
        )
        g_cumul = g_query_dec * query_f - g_key_dec * key_f - end_part
        g_cumul = g_cumul + jnp.where(last, at_stop, 0.0)
        gdecay_ref[:, ks] = lax.dot_general(
            suffix, g_cumul, (NN, ((), ())), precision=highest, preferred_element_type=jnp.float32
        )
        back_ref[vs, :] = (back_f * whole + product(grad, query_dec, TN)) * keep


def rows_spec(width, index):
    return pl.BlockSpec((BLOCK, width), index)


def mix_forward(start, qkv, cumul, incoming):
    count = qkv.shape[0] // BLOCK
    place = lambda i, s: (i, 0)
    return pl.pallas_call(
        forward_kernel,
        grid_spec=pltpu.PrefetchScalarGridSpec(
            num_scalar_prefetch=1,
            grid=(count,),
            in_specs=[
                rows_spec(2 * KD + VD, place),
                rows_spec(KD, place),
                pl.BlockSpec((VD, DK), lambda i, s: (0, 0)),
            ],
            out_specs=[
                rows_spec(VD, place),
                pl.BlockSpec((1, VD, DK), lambda i, s: (i, 0, 0)),
            ],
            scratch_shapes=[pltpu.VMEM((VD, DK), jnp.float32)],
        ),
        out_shape=[
            jax.ShapeDtypeStruct((count * BLOCK, VD), jnp.float32),
            jax.ShapeDtypeStruct((count, VD, DK), jnp.float32),
        ],
        name="mix_forward",
    )(start, qkv, cumul, incoming)


def mix_backward(start, qkv, cumul, grad, saved, outgoing):
    count = qkv.shape[0] // BLOCK
    place = lambda i, s: (count - 1 - i, 0)
    return pl.pallas_call(
        backward_kernel,
        grid_spec=pltpu.PrefetchScalarGridSpec(
            num_scalar_prefetch=1,
            grid=(count,),
            in_specs=[
                rows_spec(2 * KD + VD, place),
                rows_spec(KD, place),
                rows_spec(VD, place),
                pl.BlockSpec((1, VD, DK), lambda i, s: (count - 1 - i, 0, 0)),
                pl.BlockSpec((VD, DK), lambda i, s: (0, 0)),
            ],
            out_specs=[
                rows_spec(2 * KD + VD, place),
                rows_spec(KD, place),
            ],
            scratch_shapes=[pltpu.VMEM((VD, DK), jnp.float32)],
        ),
        out_shape=[
            jax.ShapeDtypeStruct((count * BLOCK, 2 * KD + VD), jnp.bfloat16),
            jax.ShapeDtypeStruct((count * BLOCK, KD), jnp.float32),
        ],
        name="mix_backward",
    )(start, qkv, cumul, grad, saved, outgoing)


def chain(pieces, decays, reverse):
    count = pieces.shape[0]

    def kernel(pieces_ref, decays_ref, out_ref):
        def one(step, state):
            at = count - 1 - step if reverse else step
            out_ref[at] = state.astype(jnp.bfloat16)
            return decays_ref[at] * state + pieces_ref[at].astype(jnp.float32)

        lax.fori_loop(0, count, one, jnp.zeros(pieces.shape[1:], jnp.float32))

    return pl.pallas_call(
        kernel,
        out_shape=jax.ShapeDtypeStruct(pieces.shape, jnp.bfloat16),
        name="chain_back" if reverse else "chain",
    )(pieces, decays)


def exchange(state, decay_all, reverse):
    count = decay_all.shape[0]
    rows = VD // count
    mine = lax.axis_index(EVERY)
    head = mine * rows // VALUE_WIDTH
    pieces = lax.all_to_all(state.astype(jnp.bfloat16).reshape(count, rows, DK), EVERY, 0, 0)
    decays = lax.dynamic_slice_in_dim(decay_all, head * DK, DK, 1)[:, None, :]
    folded = chain(pieces, decays, reverse)
    return lax.all_to_all(folded, EVERY, 0, 0).reshape(VD, DK)


def fetch(shard):
    piece = shard.shape[0] // lax.axis_size("replica")
    mine = lax.dynamic_slice_in_dim(shard, lax.axis_index("replica") * piece, piece, 0)
    return lax.all_gather(mine, ROWS, axis=0, tiled=True)


def reduce_rows(term):
    return lax.psum_scatter(term.astype(jnp.bfloat16), ROWS, scatter_dimension=0, tiled=True)


def gather_rows(part):
    return lax.all_gather(part, "replica", axis=0, tiled=True)


def column(vector, rows):
    return jnp.pad(vector, (0, rows - vector.shape[0]))[:, None]


def per_device(
    tokens,
    seq_start,
    out_grad,
    norm_gain,
    w_query,
    w_key,
    w_value,
    w_outgate,
    w_lowrank,
    w_rank_up,
    gate_bias,
    head_gain,
    w_output,
    ffn_gain,
    w_gate,
    w_up,
    w_down,
):
    shards = lax.axis_size("shard")
    rows = w_query.shape[0]
    rank = w_lowrank.shape[1]
    spread = w_rank_up.size // rows
    at_norm = rank
    at_ffn = rank + 1
    at_bias = rank + 2
    at_head = rank + 3
    at_up = rank + 4
    side = jnp.concatenate(
        [
            w_lowrank,
            norm_gain[:, None],
            ffn_gain[:, None],
            column(gate_bias, rows),
            column(head_gain, rows),
            w_rank_up.reshape(rows, spread),
            jnp.zeros((rows, SIDE - at_up - spread), jnp.bfloat16),
        ],
        axis=1,
    )
    mixer_w = fetch(jnp.concatenate([w_query, w_key, w_value, w_outgate, side], axis=1))
    output_w = fetch(w_output)
    gate_up_w = fetch(jnp.concatenate([w_gate, w_up], axis=1))
    down_w = fetch(w_down)

    qkv_width = 2 * KD + VD
    wide = qkv_width + VD
    side_w = mixer_w[:, wide:]
    lowrank_w = side_w[:, :rank]
    gain_one = side_w[:, at_norm].astype(jnp.float32)
    gain_two = side_w[:, at_ffn].astype(jnp.float32)
    bias_full = side_w[:, at_bias].reshape(shards, rows)[:, : gate_bias.shape[0]].reshape(-1)
    head_one = (
        side_w[:, at_head].reshape(shards, rows)[:, : head_gain.shape[0]].reshape(-1)
    ).astype(jnp.float32)
    rank_up_w = side_w[:, at_up : at_up + spread].reshape(rank, KD)

    residual_in = tokens.astype(jnp.float32)
    count_of_rows = residual_in.shape[0]
    block_count = count_of_rows // BLOCK
    slice_start = seq_start[0]
    normed = rms_norm(residual_in, gain_one).astype(jnp.bfloat16)
    qkv = dense(normed, mixer_w[:, :qkv_width]).astype(jnp.bfloat16)
    outgate = dense(normed, mixer_w[:, qkv_width:wide])
    rank_rows = dense(normed, lowrank_w).astype(jnp.bfloat16)
    gate_logit = dense(rank_rows, rank_up_w) + bias_full.astype(jnp.float32)
    log_decay = jax.nn.log_sigmoid(gate_logit) / normalizer

    lower = jnp.tril(jnp.ones((BLOCK, BLOCK), jnp.float32))
    cumul3 = jnp.einsum(
        "ij,bjk->bik", lower, log_decay.reshape(block_count, BLOCK, KD), precision=highest
    )
    stops = cumul3[:, -1]
    strict = jnp.tril(jnp.ones((block_count, block_count), jnp.float32), -1)
    ahead_of = jnp.dot(strict, stops, precision=highest)
    after = jnp.dot(strict.T, stops, precision=highest)
    cumul = cumul3.reshape(count_of_rows, KD)
    query_f = qkv[:, :KD].astype(jnp.float32)
    key_f = qkv[:, KD : 2 * KD].astype(jnp.float32)
    value_rows = qkv[:, 2 * KD :]
    has_start = slice_start < count_of_rows
    at = jnp.arange(count_of_rows, dtype=jnp.int32)[:, None]
    to_end = jnp.exp((stops + after)[:, None, :] - cumul3).reshape(count_of_rows, KD)
    counts = jnp.logical_or(jnp.logical_not(has_start), at >= slice_start)
    key_to_end = jnp.where(counts, key_f * to_end, 0.0)
    from_first = jnp.exp(ahead_of[:, None, :] + cumul3).reshape(count_of_rows, KD)
    query_first = jnp.where(at < slice_start, query_f * from_first, 0.0)
    carry_decay = jnp.where(has_start, 0.0, jnp.exp(jnp.sum(stops, axis=0)))
    decay_all = lax.all_gather(carry_decay, EVERY)

    def heads(rows_of, width):
        return rows_of.reshape(count_of_rows, HEAD_COUNT, width)

    local_end = jnp.einsum(
        "thv,thk->hvk",
        heads(value_rows.astype(jnp.float32), VALUE_WIDTH),
        heads(key_to_end, DK),
        precision=high,
    ).reshape(VD, DK)
    incoming = exchange(local_end, decay_all, False)
    mixed_rows, saved = mix_forward(seq_start, qkv, cumul, incoming)
    gated_rows = output_gate(mixed_rows, outgate, head_one).astype(jnp.bfloat16)
    middle = residual_in + dense(gated_rows, output_w)
    normed_ffn = rms_norm(middle, gain_two).astype(jnp.bfloat16)
    width = w_gate.shape[1]
    gate_w = gate_up_w[:, :width]
    up_w = gate_up_w[:, width:]
    gate_pre = dense(normed_ffn, gate_w)
    up_pre = dense(normed_ffn, up_w)
    hidden = swiglu(gate_pre, up_pre).astype(jnp.bfloat16)
    output = (middle + dense(hidden, down_w)).astype(jnp.bfloat16)

    grad_out = out_grad.astype(jnp.float32)
    part_down = reduce_rows(dense_left(hidden, out_grad))
    grad_hidden = dense_back(out_grad, down_w)
    unused, pull_swiglu = jax.vjp(swiglu, gate_pre, up_pre)
    grad_gate_f, grad_up_f = pull_swiglu(grad_hidden)
    grad_both = jnp.concatenate(
        [grad_gate_f.astype(jnp.bfloat16), grad_up_f.astype(jnp.bfloat16)], axis=1
    )
    grad_both, term_both = lax.optimization_barrier(
        (grad_both, dense_left(normed_ffn, grad_both).astype(jnp.bfloat16))
    )
    part_both = reduce_rows(term_both)
    grad_normed_ffn = dense_back(grad_both, gate_up_w)
    unused, pull_norm_two = jax.vjp(rms_norm, middle, gain_two)
    grad_middle_part, grad_gain_two = pull_norm_two(grad_normed_ffn)
    grad_middle = grad_out + grad_middle_part
    grad_attn = grad_middle.astype(jnp.bfloat16)
    grad_attn, term_output = lax.optimization_barrier(
        (grad_attn, dense_left(gated_rows, grad_attn).astype(jnp.bfloat16))
    )
    part_output = reduce_rows(term_output)
    grad_gated = dense_back(grad_attn, output_w)
    unused, pull_gate = jax.vjp(output_gate, mixed_rows, outgate, head_one)
    mixed_gradient, grad_outgate_f, grad_head = pull_gate(grad_gated)
    grad_outgate = grad_outgate_f.astype(jnp.bfloat16)
    carry_grad = jnp.einsum(
        "thv,thk->hvk",
        heads(mixed_gradient, VALUE_WIDTH),
        heads(query_first, DK),
        precision=high,
    ).reshape(VD, DK)
    outgoing = exchange(carry_grad, decay_all, True)
    grad_qkv, grad_decay = mix_backward(
        seq_start, qkv, cumul, mixed_gradient, saved, outgoing
    )
    grad_logit = (grad_decay * jax.nn.sigmoid(-gate_logit) / normalizer).astype(jnp.bfloat16)
    grad_bias = jnp.sum(grad_logit.astype(jnp.float32), axis=0)
    grad_rank_up = dense_left(rank_rows, grad_logit)
    grad_rank = dense_back(grad_logit, rank_up_w).astype(jnp.bfloat16)
    grad_mixer = jnp.concatenate(
        [grad_qkv, grad_outgate, jnp.pad(grad_rank, ((0, 0), (0, SIDE - rank)))], axis=1
    )
    grad_normed = dense_back(grad_mixer, mixer_w)
    unused, pull_norm_one = jax.vjp(rms_norm, residual_in, gain_one)
    grad_input_part, grad_gain_one = pull_norm_one(grad_normed)
    grad_tokens = (grad_middle + grad_input_part).astype(jnp.bfloat16)

    def spread_rows(vector):
        per = vector.reshape(shards, -1)
        return jnp.pad(per, ((0, 0), (0, rows - per.shape[1]))).reshape(-1, 1)

    small = jnp.concatenate(
        [
            grad_gain_one[:, None],
            grad_gain_two[:, None],
            spread_rows(grad_bias),
            spread_rows(grad_head),
            grad_rank_up.reshape(shards * rows, spread),
        ],
        axis=1,
    )
    term = dense_left(normed, grad_mixer)
    term = term + jnp.pad(small, ((0, 0), (wide + rank, SIDE - rank - small.shape[1])))
    term, part_down, part_both, part_output = lax.optimization_barrier(
        (term.astype(jnp.bfloat16), part_down, part_both, part_output)
    )
    sum_down = gather_rows(part_down)
    sum_both = gather_rows(part_both)
    sum_output = gather_rows(part_output)
    sum_mixer = gather_rows(reduce_rows(term))

    def final(part):
        return part.astype(jnp.float32)

    side_sum = sum_mixer[:, wide:]
    return (
        output,
        grad_tokens,
        final(side_sum[:, at_norm]),
        final(sum_mixer[:, :KD]),
        final(sum_mixer[:, KD : 2 * KD]),
        final(sum_mixer[:, 2 * KD : qkv_width]),
        final(sum_mixer[:, qkv_width:wide]),
        final(side_sum[:, :rank]),
        final(side_sum[:, at_up : at_up + spread].reshape(w_rank_up.shape)),
        final(side_sum[: gate_bias.shape[0], at_bias]),
        final(side_sum[: head_gain.shape[0], at_head]),
        final(sum_output),
        final(side_sum[:, at_ffn]),
        final(sum_both[:, :width]),
        final(sum_both[:, width:]),
        final(sum_down),
    )


def solution(mesh):
    return jax.shard_map(
        per_device,
        mesh=mesh,
        in_specs=(
            P(("replica", "shard"), None),
            P(("replica", "shard")),
            P(("replica", "shard"), None),
            P("shard"),
            P("shard", None),
            P("shard", None),
            P("shard", None),
            P("shard", None),
            P("shard", None),
            P("shard", None),
            P("shard"),
            P("shard"),
            P("shard", None),
            P("shard"),
            P("shard", None),
            P("shard", None),
            P("shard", None),
        ),
        out_specs=(
            P(("replica", "shard"), None),
            P(("replica", "shard"), None),
            P("shard"),
            P("shard", None),
            P("shard", None),
            P("shard", None),
            P("shard", None),
            P("shard", None),
            P("shard", None),
            P("shard"),
            P("shard"),
            P("shard", None),
            P("shard"),
            P("shard", None),
            P("shard", None),
            P("shard", None),
        ),
        check_vma=False,
    )
```
